128 devices in a mesh: param: 16 (over x, y_hi, core), ex: 8 (over y_lo, z).
Axes of the slice: x: 4, y: 4 (y_hi: 2, y_lo: 2; y = y_hi * 2 + y_lo), z: 4, core: 2. Of those that a mesh axis runs over, the one named last changes fastest.
Arguments:
- grads: float32 [98304, 4096], P('param', 'ex'), may hold values from -6 to 6
- projection: bfloat16 [98304, 1024], P('param'), may hold values from -6 to 6
- whitener: float32 [1024, 1024], P('param'), may hold values from -1 to 3
Outputs:
- scores: float32 [4096, 4096], P('ex', 'param')
The draws below stay inside these ranges and needn't reach their ends.
All inputs are finite; a program needn't handle non-finite values.
Results may differ from the reference program's by a relative error of at most 0.0052.
Values may be sent and summed in bfloat16 or wider, within the bound.
No kernel may reach another device: no remote copies, remote signals or barrier semaphores. Data moves between devices by JAX's collectives and lax.ppermute only.
A program may use at most 128 MiB of HBM per device.

```python
import math
import jax
import jax.numpy as jnp
from jax import lax

K = 1024
PARAMS = 98304
EXAMPLES = 4096


def draw_whitener(key, part):
    first_key = jax.random.fold_in(key, 11)
    second_key = jax.random.fold_in(key, 23)
    diagonal = jnp.exp(jax.random.uniform(first_key, (K,), jnp.float32, -0.7, 0.7))
    off_part = jax.random.normal(second_key, (K, K), jnp.float32) * (0.5 / jnp.sqrt(1.0 * K))
    off_part = jnp.clip(off_part, -0.9, 0.9)
    return off_part + jnp.diag(diagonal)


def level_of(rng, extent, split, least, largest):
    def one(dim, blocks):
        steps = jax.random.uniform(jax.random.fold_in(jax.random.fold_in(rng, 6), dim), (blocks,), jnp.float32, least / len(split), largest / len(split))
        return jnp.repeat(jnp.exp(steps), extent[dim] // blocks).reshape((-1,) + (1,) * (len(extent) - dim - 1))

    gain = one(*split[0])
    for cut in split[1:]:
        gain = gain * one(*cut)
    return gain


def noise(stream_key, dims, scale, most, split=(), dtype=jnp.bfloat16):
    drawn = scale * jax.random.normal(stream_key, dims, jnp.float32)
    if split:
        drawn = drawn * level_of(stream_key, dims, split, -0.22, 0.18)
    return jnp.clip(drawn, -most, most).astype(dtype)


def setup_inputs(seed: int = 0) -> dict:
    keys = jax.random.split(jax.random.key(seed), 4)
    return {
        "grads": noise(keys[0], (PARAMS, EXAMPLES), 1.0, 6.0, ((0, 16), (1, 8)), jnp.float32),
        "projection": noise(keys[1], (PARAMS, K), 1.0, 6.0, ((0, 16),)),
        "whitener": draw_whitener(jax.random.fold_in(keys[3], 71), 0),
    }


def reference(grads, projection, whitener):
    low_grads = grads.astype(jnp.bfloat16)
    sketch = jnp.dot(projection.T, low_grads, preferred_element_type=jnp.float32) * (1.0 / math.sqrt(PARAMS))
    whitened = jnp.dot(whitener, sketch, precision=lax.Precision.HIGHEST).astype(jnp.bfloat16)
    return jnp.dot(whitened.T, whitened, preferred_element_type=jnp.float32) / K
```

```python
import math

import jax
import jax.numpy as jnp
from jax import lax
from jax.sharding import Mesh, PartitionSpec as P

BF16 = jnp.bfloat16
F32 = jnp.float32
RING = ("x", "y_hi")
COLS = ("y_lo", "z")


def matmul(a, b, dims):
    return lax.dot_general(a, b, (dims, ((), ())), preferred_element_type=F32)


def gather(block, axes):
    n = lax.axis_size(axes)
    copies = jnp.broadcast_to(block[None], (n,) + block.shape)
    return lax.all_to_all(copies, axes, 0, 0, tiled=True)


def body(grads, projection, whitener):
    n = lax.axis_size(RING)
    core = lax.axis_index("core")
    sketch_rows = projection.shape[1]
    norm_factor = 1.0 / math.sqrt(grads.shape[0] * n * lax.axis_size("core"))
    width = grads.shape[1]
    half = width // 2

    whole = lax.all_gather(whitener.astype(BF16), ("x", "y_hi", "core"), axis=0, tiled=True)

    partial = matmul(grads.astype(BF16), projection, ((0,), (0,)))
    keep = lax.dynamic_slice_in_dim(partial, core * half, half, 0)
    give = lax.dynamic_slice_in_dim(partial, (1 - core) * half, half, 0).astype(BF16)
    swap = [(0, 1), (1, 0)]
    chip = keep + lax.ppermute(give, "core", swap).astype(F32)
    blocks = chip.astype(BF16).reshape(n, half // n, sketch_rows)
    pieces = lax.all_to_all(blocks, RING, 0, 0, tiled=True)
    sketch = (jnp.sum(pieces.astype(F32), axis=0) * norm_factor).astype(BF16)
    white = matmul(sketch, whole, ((1,), (1,))).astype(BF16)

    turn = [(q * n + e, e * n + q) for e in range(n) for q in range(n)]
    other = lax.ppermute(white, RING + COLS, turn)
    row_half = gather(white, RING).reshape(half, sketch_rows)
    row_other = lax.ppermute(row_half, "core", swap)
    cols = gather(other, COLS).reshape(half, sketch_rows)
    own = matmul(row_half, cols, ((1,), (1,)))
    far = matmul(row_other, cols, ((1,), (1,)))
    first = jnp.where(core == 0, own, far)
    second = jnp.where(core == 0, far, own)
    return jnp.concatenate([first, second], axis=0) * (1.0 / sketch_rows)


def solution(mesh):
    fine = Mesh(mesh.devices.reshape(4, 2, 2, 2, 4), ("x", "y_hi", "core", "y_lo", "z"))
    param = ("x", "y_hi", "core")
    return jax.shard_map(
        body,
        mesh=fine,
        in_specs=(P(param, COLS), P(param, None), P(param, None)),
        out_specs=P(COLS, param),
        check_vma=False,
    )
```

```python
import math

import jax
import jax.numpy as jnp
from jax import lax
from jax.experimental import pallas as pl
from jax.experimental.pallas import tpu as pltpu
from jax.sharding import Mesh, PartitionSpec as P

BF16 = jnp.bfloat16
F32 = jnp.float32
RING = ("x", "y_hi")
COLS = ("y_lo", "z")
SWAP = [(0, 1), (1, 0)]
TILE = 512
STEPS = (1, 2, 3, 3, 2, 1)


def matmul(a, b, dims):
    return lax.dot_general(a, b, (dims, ((), ())), preferred_element_type=F32)


def send_all(copies, axes):
    return lax.all_to_all(copies, axes, 0, 0, tiled=True)


def project_kernel(
    core_ref, grads_hbm, projection_hbm, keep_ref, give_ref, grads_ref, projection_ref, total, sems
):
    rows = grads_ref.shape[0]
    half = keep_ref.shape[1]
    copies = []
    for i in range(rows // TILE):
        part = pl.ds(i * TILE, TILE)
        pair = (
            pltpu.make_async_copy(grads_hbm.at[part], grads_ref.at[part], sems.at[0, i]),
            pltpu.make_async_copy(projection_hbm.at[part], projection_ref.at[part], sems.at[1, i]),
        )
        for copy in pair:
            copy.start()
        copies.append(pair)
    first = 0
    for count in STEPS:
        for pair in copies[first : first + count]:
            for copy in pair:
                copy.wait()
        part = pl.ds(first * TILE, count * TILE)
        term = matmul(grads_ref[part, :].astype(BF16), projection_ref[part, :], ((0,), (0,)))
        if first == 0:
            total[...] = term
        else:
            total[...] += term
        first += count
    mine = pl.multiple_of(core_ref[0] * half, half)
    theirs = pl.multiple_of((1 - core_ref[0]) * half, half)
    keep_ref[...] = total[:, pl.ds(mine, half)]
    give_ref[...] = total[:, pl.ds(theirs, half)].astype(BF16)


def project(core, grads, projection):
    rows, width = grads.shape
    cols = projection.shape[1]
    half = cols // 2
    hbm = pl.BlockSpec(memory_space=pl.ANY)
    vmem = pl.BlockSpec(memory_space=pltpu.VMEM)
    return pl.pallas_call(
        project_kernel,
        out_shape=(
            jax.ShapeDtypeStruct((width, half), F32),
            jax.ShapeDtypeStruct((width, half), BF16),
        ),
        in_specs=[pl.BlockSpec(memory_space=pltpu.SMEM), hbm, hbm],
        out_specs=[vmem, vmem],
        scratch_shapes=[
            pltpu.VMEM((rows, width), grads.dtype),
            pltpu.VMEM((rows, cols), projection.dtype),
            pltpu.VMEM((width, cols), F32),
            pltpu.SemaphoreType.DMA((2, rows // TILE)),
        ],
        compiler_params=pltpu.CompilerParams(vmem_limit_bytes=52 << 20),
        cost_estimate=pl.CostEstimate(
            flops=2 * rows * width * cols,
            bytes_accessed=rows * (4 * width + 2 * cols),
            transcendentals=0,
        ),
        name="project",
    )(core, grads, projection)


def spread_kernel(part_ref, out_ref):
    part = part_ref[...].astype(BF16)
    for i in range(out_ref.shape[0]):
        out_ref[i] = part


def spread(part, count):
    return pl.pallas_call(
        spread_kernel,
        out_shape=jax.ShapeDtypeStruct((count,) + part.shape, BF16),
        in_specs=[pl.BlockSpec(memory_space=pltpu.VMEM)],
        out_specs=pl.BlockSpec(memory_space=pltpu.VMEM),
        name="spread",
    )(part)


def call(kernel, out_shape, flops, *args, scratch=(), name):
    vmem = pl.BlockSpec(memory_space=pltpu.VMEM)
    moved = sum(a.size * a.dtype.itemsize for a in args[1:])
    return pl.pallas_call(
        kernel,
        out_shape=out_shape,
        in_specs=[pl.BlockSpec(memory_space=pltpu.SMEM)] + [vmem] * (len(args) - 1),
        out_specs=jax.tree.map(lambda _: vmem, out_shape),
        scratch_shapes=scratch,
        compiler_params=pltpu.CompilerParams(vmem_limit_bytes=24 << 20),
        cost_estimate=pl.CostEstimate(flops=flops, bytes_accessed=moved, transcendentals=0),
        name=name,
    )(*args)


def reduce_kernel(core_ref, pieces_ref, out_ref, *, groups, scale):
    count, rows, _ = pieces_ref.shape
    for e in range(groups):
        total = pieces_ref[e].astype(F32)
        for q in range(1, count // groups):
            total += pieces_ref[q * groups + e].astype(F32)
        out_ref[e * rows : (e + 1) * rows, :] = total * scale


def whiten_kernel(core_ref, mine_ref, theirs_ref, whitener_ref, out_ref):
    rows, half = mine_ref.shape
    total = jnp.zeros((rows, whitener_ref.shape[0]), F32)
    for ref, side in ((mine_ref, core_ref[0]), (theirs_ref, 1 - core_ref[0])):
        part = ref[...]
        high = part.astype(BF16)
        low = (part - high.astype(F32)).astype(BF16)
        block = whitener_ref[:, pl.ds(pl.multiple_of(side * half, half), half)]
        term = matmul(jnp.concatenate([high, low], axis=0), block, ((1,), (1,)))
        total += term[:rows] + term[rows:]
    white = total.astype(BF16)
    size = out_ref.shape[1] // 2
    n = rows // size
    for q in range(n):
        for e in range(n):
            out_ref[q * n + e, :size, :] = white[e * size : (e + 1) * size]
            out_ref[q * n + e, size:, :] = white[q * size : (q + 1) * size]


def score_kernel(core_ref, pieces_ref, keep_ref, give_ref, rows_ref, cols_ref):
    count, size, _ = pieces_ref.shape
    size //= 2
    for i in range(count):
        rows_ref[i * size : (i + 1) * size, :] = pieces_ref[i, :size, :]
        cols_ref[i * size : (i + 1) * size, :] = pieces_ref[i, size:, :]
    half = keep_ref.shape[1]
    mine = pl.multiple_of(core_ref[0] * half, half)
    theirs = pl.multiple_of((1 - core_ref[0]) * half, half)
    rows = rows_ref[...]
    give_ref[...] = matmul(rows, cols_ref[pl.ds(theirs, half), :], ((1,), (1,))).astype(BF16)
    keep_ref[...] = matmul(rows, cols_ref[pl.ds(mine, half), :], ((1,), (1,)))


def body(grads, projection, whitener):
    n = lax.axis_size(RING)
    chips = RING + COLS
    core = lax.axis_index("core").astype(jnp.int32).reshape(1)
    sketch_rows = projection.shape[1]
    norm_factor = 1.0 / math.sqrt(grads.shape[0] * n * lax.axis_size("core"))
    width = grads.shape[1]
    half = sketch_rows // 2
    size = width // (n * n)

    own = send_all(spread(whitener, n), RING).reshape(half, sketch_rows)

    keep, give = project(core, grads, projection)
    got = lax.ppermute(give, "core", SWAP)
    got, own = lax.optimization_barrier((got, own))
    blocks = (keep + got.astype(F32)).astype(BF16)
    pieces = send_all(blocks.reshape(n * n, size, half), chips)
    shape = jax.ShapeDtypeStruct((n * size, half), F32)
    mine = call(
        lambda *refs: reduce_kernel(*refs, groups=n, scale=norm_factor),
        shape, 0, core, pieces, name="reduce",
    )
    theirs = lax.ppermute(mine, "core", SWAP)
    shape = jax.ShapeDtypeStruct((n * n, 2 * size, half), BF16)
    flops = 4 * n * size * sketch_rows * half
    copies = call(whiten_kernel, shape, flops, core, mine, theirs, own, name="whiten")
    pieces = send_all(copies, chips)
    side = lax.axis_size("core")
    shapes = (
        jax.ShapeDtypeStruct((width, width // side), F32),
        jax.ShapeDtypeStruct((width, width // side), BF16),
    )
    flops = 2 * width * width * half
    scratch = [pltpu.VMEM((width, half), BF16)] * 2
    keep, give = call(score_kernel, shapes, flops, core, pieces, scratch=scratch, name="score")
    got = lax.ppermute(give, "core", SWAP)
    return (keep + got.astype(F32)) * (1.0 / sketch_rows)


def solution(mesh):
    fine = Mesh(mesh.devices.reshape(4, 2, 2, 2, 4), ("x", "y_hi", "core", "y_lo", "z"))
    param = ("x", "y_hi", "core")
    return jax.shard_map(
        body,
        mesh=fine,
        in_specs=(P(param, COLS), P(param, None), P(param, None)),
        out_specs=P(COLS, param),
        check_vma=False,
    )
```

```python
import math

import jax
import jax.numpy as jnp
from jax import lax
from jax.experimental import pallas as pl
from jax.experimental.pallas import tpu as pltpu
from jax.sharding import Mesh, PartitionSpec as P

BF16 = jnp.bfloat16
F32 = jnp.float32
RING = ("x", "y_hi")
COLS = ("y_lo", "z")
SWAP = [(0, 1), (1, 0)]
TILE = 512
STEPS = (1, 2, 3, 3, 2, 1)


def matmul(a, b, dims):
    return lax.dot_general(a, b, (dims, ((), ())), preferred_element_type=F32)


def send_all(copies, axes):
    return lax.all_to_all(copies, axes, 0, 0, tiled=True)


def project_kernel(
    core_ref, grads_hbm, projection_hbm, keep_ref, give_ref, grads_ref, projection_ref, total, sems
):
    rows = grads_ref.shape[0]
    half = keep_ref.shape[1]
    mine = pl.ds(pl.multiple_of(core_ref[0] * half, half), half)
    theirs = pl.ds(pl.multiple_of((1 - core_ref[0]) * half, half), half)
    copies = []
    for i in range(rows // TILE):
        part = pl.ds(i * TILE, TILE)
        pair = (
            pltpu.make_async_copy(grads_hbm.at[part], grads_ref.at[part], sems.at[0, i]),
            pltpu.make_async_copy(projection_hbm.at[part], projection_ref.at[part], sems.at[1, i]),
        )
        for copy in pair:
            copy.start()
        copies.append(pair)
    first = 0
    for count in STEPS:
        for pair in copies[first : first + count]:
            for copy in pair:
                copy.wait()
        part = pl.ds(first * TILE, count * TILE)
        grads = grads_ref[part, :].astype(BF16)
        near = matmul(grads, projection_ref[part, mine], ((0,), (0,)))
        far = matmul(grads, projection_ref[part, theirs], ((0,), (0,)))
        first += count
        if first == count:
            keep_ref[...] = near
            total[...] = far
        elif first < rows // TILE:
            keep_ref[...] += near
            total[...] += far
        else:
            keep_ref[...] += near
            give_ref[...] = (total[...] + far).astype(BF16)


def project(core, grads, projection):
    rows, width = grads.shape
    cols = projection.shape[1]
    half = cols // 2
    hbm = pl.BlockSpec(memory_space=pl.ANY)
    vmem = pl.BlockSpec(memory_space=pltpu.VMEM)
    return pl.pallas_call(
        project_kernel,
        out_shape=(
            jax.ShapeDtypeStruct((width, half), F32),
            jax.ShapeDtypeStruct((width, half), BF16),
        ),
        in_specs=[pl.BlockSpec(memory_space=pltpu.SMEM), hbm, hbm],
        out_specs=[vmem, vmem],
        scratch_shapes=[
            pltpu.VMEM((rows, width), grads.dtype),
            pltpu.VMEM((rows, cols), projection.dtype),
            pltpu.VMEM((width, half), F32),
            pltpu.SemaphoreType.DMA((2, rows // TILE)),
        ],
        compiler_params=pltpu.CompilerParams(vmem_limit_bytes=52 << 20),
        cost_estimate=pl.CostEstimate(
            flops=2 * rows * width * cols,
            bytes_accessed=rows * (4 * width + 2 * cols),
            transcendentals=0,
        ),
        name="project",
    )(core, grads, projection)


def spread_kernel(part_ref, out_ref):
    part = part_ref[...].astype(BF16)
    for i in range(out_ref.shape[0]):
        out_ref[i] = part


def spread(part, count):
    return pl.pallas_call(
        spread_kernel,
        out_shape=jax.ShapeDtypeStruct((count,) + part.shape, BF16),
        in_specs=[pl.BlockSpec(memory_space=pltpu.VMEM)],
        out_specs=pl.BlockSpec(memory_space=pltpu.VMEM),
        name="spread",
    )(part)


def call(kernel, out_shape, flops, *args, scratch=(), name):
    vmem = pl.BlockSpec(memory_space=pltpu.VMEM)
    moved = sum(a.size * a.dtype.itemsize for a in args[1:])
    return pl.pallas_call(
        kernel,
        out_shape=out_shape,
        in_specs=[pl.BlockSpec(memory_space=pltpu.SMEM)] + [vmem] * (len(args) - 1),
        out_specs=jax.tree.map(lambda _: vmem, out_shape),
        scratch_shapes=scratch,
        compiler_params=pltpu.CompilerParams(vmem_limit_bytes=24 << 20),
        cost_estimate=pl.CostEstimate(flops=flops, bytes_accessed=moved, transcendentals=0),
        name=name,
    )(*args)


def reduce_kernel(core_ref, pieces_ref, out_ref, *, groups, scale):
    count, rows, _ = pieces_ref.shape
    for e in range(groups):
        total = pieces_ref[e].astype(F32)
        for q in range(1, count // groups):
            total += pieces_ref[q * groups + e].astype(F32)
        out_ref[e * rows : (e + 1) * rows, :] = total * scale


def whiten_half(part, block):
    rows = part.shape[0]
    high = part.astype(BF16)
    low = (part - high.astype(F32)).astype(BF16)
    term = matmul(jnp.concatenate([high, low], axis=0), block, ((1,), (1,)))
    return term[:rows] + term[rows:]


def first_half_kernel(core_ref, mine_ref, whitener_ref, out_ref):
    half = mine_ref.shape[1]
    mine = pl.ds(pl.multiple_of(core_ref[0] * half, half), half)
    out_ref[...] = whiten_half(mine_ref[...], whitener_ref[:, mine])


def whiten_kernel(core_ref, first_ref, theirs_ref, whitener_ref, out_ref):
    rows, half = theirs_ref.shape
    theirs = pl.ds(pl.multiple_of((1 - core_ref[0]) * half, half), half)
    white = (first_ref[...] + whiten_half(theirs_ref[...], whitener_ref[:, theirs])).astype(BF16)
    size = out_ref.shape[1] // 2
    n = rows // size
    for q in range(n):
        for e in range(n):
            out_ref[q * n + e, :size, :] = white[e * size : (e + 1) * size]
            out_ref[q * n + e, size:, :] = white[q * size : (q + 1) * size]


def give_kernel(core_ref, pieces_ref, give_ref, rows_ref, cols_ref):
    count, size, _ = pieces_ref.shape
    size //= 2
    for i in range(count):
        rows_ref[i * size : (i + 1) * size, :] = pieces_ref[i, :size, :]
        cols_ref[i * size : (i + 1) * size, :] = pieces_ref[i, size:, :]
    half = give_ref.shape[1]
    theirs = pl.ds(pl.multiple_of((1 - core_ref[0]) * half, half), half)
    give_ref[...] = matmul(rows_ref[...], cols_ref[theirs, :], ((1,), (1,))).astype(BF16)


def keep_kernel(core_ref, rows_ref, cols_ref, keep_ref):
    half = keep_ref.shape[1]
    mine = pl.ds(pl.multiple_of(core_ref[0] * half, half), half)
    keep_ref[...] = matmul(rows_ref[...], cols_ref[mine, :], ((1,), (1,)))


def body(grads, projection, whitener):
    n = lax.axis_size(RING)
    chips = RING + COLS
    core = lax.axis_index("core").astype(jnp.int32).reshape(1)
    sketch_rows = projection.shape[1]
    norm_factor = 1.0 / math.sqrt(grads.shape[0] * n * lax.axis_size("core"))
    width = grads.shape[1]
    half = sketch_rows // 2
    size = width // (n * n)

    own = send_all(spread(whitener, n), RING).reshape(half, sketch_rows)

    keep, give = project(core, grads, projection)
    got = lax.ppermute(give, "core", SWAP)
    got, own = lax.optimization_barrier((got, own))
    blocks = (keep + got.astype(F32)).astype(BF16)
    pieces = send_all(blocks.reshape(n * n, size, half), chips)
    shape = jax.ShapeDtypeStruct((n * size, half), F32)
    mine = call(
        lambda *refs: reduce_kernel(*refs, groups=n, scale=norm_factor),
        shape, 0, core, pieces, name="reduce",
    )
    theirs = lax.ppermute(mine, "core", SWAP)
    flops = 4 * n * size * half * half
    shape = jax.ShapeDtypeStruct((n * size, half), F32)
    first = call(first_half_kernel, shape, flops, core, mine, own, name="first_half")
    shape = jax.ShapeDtypeStruct((n * n, 2 * size, half), BF16)
    copies = call(whiten_kernel, shape, flops, core, first, theirs, own, name="whiten")
    pieces = send_all(copies, chips)
    across = width // lax.axis_size("core")
    flops = 2 * width * across * half
    shapes = (
        jax.ShapeDtypeStruct((width, across), BF16),
        jax.ShapeDtypeStruct((width, half), BF16),
        jax.ShapeDtypeStruct((width, half), BF16),
    )
    give, rows, cols = call(give_kernel, shapes, flops, core, pieces, name="give")
    got = lax.ppermute(give, "core", SWAP)
    shape = jax.ShapeDtypeStruct((width, across), F32)
    keep = call(keep_kernel, shape, flops, core, rows, cols, name="keep")
    return (keep + got.astype(F32)) * (1.0 / sketch_rows)


def solution(mesh):
    fine = Mesh(mesh.devices.reshape(4, 2, 2, 2, 4), ("x", "y_hi", "core", "y_lo", "z"))
    param = ("x", "y_hi", "core")
    return jax.shard_map(
        body,
        mesh=fine,
        in_specs=(P(param, COLS), P(param, None), P(param, None)),
        out_specs=P(COLS, param),
        check_vma=False,
    )
```

```python
import math

import jax
import jax.numpy as jnp
from jax import lax
from jax.experimental import pallas as pl
from jax.experimental.pallas import tpu as pltpu
from jax.sharding import Mesh, PartitionSpec as P

BF16 = jnp.bfloat16
F32 = jnp.float32
RING = ("x", "y_hi")
COLS = ("y_lo", "z")
SWAP = [(0, 1), (1, 0)]
TILE = 512
STEPS = (1, 2, 3, 3, 2, 1)


def matmul(a, b, dims):
    return lax.dot_general(a, b, (dims, ((), ())), preferred_element_type=F32)


def send_all(copies, axes):
    return lax.all_to_all(copies, axes, 0, 0, tiled=True)


def project_kernel(
    core_ref, grads_hbm, projection_hbm, keep_ref, give_ref, grads_ref, projection_ref, total, sems
):
    rows = grads_ref.shape[0]
    half = keep_ref.shape[1]
    mine = pl.ds(pl.multiple_of(core_ref[0] * half, half), half)
    theirs = pl.ds(pl.multiple_of((1 - core_ref[0]) * half, half), half)
    copies = []
    for i in range(rows // TILE):
        part = pl.ds(i * TILE, TILE)
        pair = (
            pltpu.make_async_copy(grads_hbm.at[part], grads_ref.at[part], sems.at[0, i]),
            pltpu.make_async_copy(projection_hbm.at[part], projection_ref.at[part], sems.at[1, i]),
        )
        for copy in pair:
            copy.start()
        copies.append(pair)
    first = 0
    for count in STEPS:
        for pair in copies[first : first + count]:
            for copy in pair:
                copy.wait()
        part = pl.ds(first * TILE, count * TILE)
        grads = grads_ref[part, :].astype(BF16)
        near = matmul(grads, projection_ref[part, mine], ((0,), (0,)))
        far = matmul(grads, projection_ref[part, theirs], ((0,), (0,)))
        first += count
        if first == count:
            keep_ref[...] = near
            total[...] = far
        elif first < rows // TILE:
            keep_ref[...] += near
            total[...] += far
        else:
            keep_ref[...] += near
            give_ref[...] = (total[...] + far).astype(BF16)


def project(core, grads, projection):
    rows, width = grads.shape
    cols = projection.shape[1]
    half = cols // 2
    hbm = pl.BlockSpec(memory_space=pl.ANY)
    vmem = pl.BlockSpec(memory_space=pltpu.VMEM)
    return pl.pallas_call(
        project_kernel,
        out_shape=(
            jax.ShapeDtypeStruct((width, half), F32),
            jax.ShapeDtypeStruct((width, half), BF16),
        ),
        in_specs=[pl.BlockSpec(memory_space=pltpu.SMEM), hbm, hbm],
        out_specs=[vmem, vmem],
        scratch_shapes=[
            pltpu.VMEM((rows, width), grads.dtype),
            pltpu.VMEM((rows, cols), projection.dtype),
            pltpu.VMEM((width, half), F32),
            pltpu.SemaphoreType.DMA((2, rows // TILE)),
        ],
        compiler_params=pltpu.CompilerParams(vmem_limit_bytes=52 << 20),
        cost_estimate=pl.CostEstimate(
            flops=2 * rows * width * cols,
            bytes_accessed=rows * (4 * width + 2 * cols),
            transcendentals=0,
        ),
        name="project",
    )(core, grads, projection)


def spread_kernel(part_ref, out_ref):
    part = part_ref[...].astype(BF16)
    for i in range(out_ref.shape[0]):
        out_ref[i] = part


def spread(part, count):
    return pl.pallas_call(
        spread_kernel,
        out_shape=jax.ShapeDtypeStruct((count,) + part.shape, BF16),
        in_specs=[pl.BlockSpec(memory_space=pltpu.VMEM)],
        out_specs=pl.BlockSpec(memory_space=pltpu.VMEM),
        name="spread",
    )(part)


def call(kernel, out_shape, flops, *args, scratch=(), name):
    vmem = pl.BlockSpec(memory_space=pltpu.VMEM)
    moved = sum(a.size * a.dtype.itemsize for a in args[1:])
    return pl.pallas_call(
        kernel,
        out_shape=out_shape,
        in_specs=[pl.BlockSpec(memory_space=pltpu.SMEM)] + [vmem] * (len(args) - 1),
        out_specs=jax.tree.map(lambda _: vmem, out_shape),
        scratch_shapes=scratch,
        compiler_params=pltpu.CompilerParams(vmem_limit_bytes=24 << 20),
        cost_estimate=pl.CostEstimate(flops=flops, bytes_accessed=moved, transcendentals=0),
        name=name,
    )(*args)


def reduce_kernel(core_ref, pieces_ref, out_ref, *, groups, scale):
    count, rows, _ = pieces_ref.shape
    for e in range(groups):
        total = pieces_ref[e].astype(F32)
        for q in range(1, count // groups):
            total += pieces_ref[q * groups + e].astype(F32)
        out_ref[e * rows : (e + 1) * rows, :] = total * scale


def whiten_half(part, block):
    rows = part.shape[0]
    high = part.astype(BF16)
    low = (part - high.astype(F32)).astype(BF16)
    term = matmul(jnp.concatenate([high, low], axis=0), block, ((1,), (1,)))
    return term[:rows] + term[rows:]


def first_half_kernel(core_ref, mine_ref, whitener_ref, out_ref):
    half = mine_ref.shape[1]
    mine = pl.ds(pl.multiple_of(core_ref[0] * half, half), half)
    out_ref[...] = whiten_half(mine_ref[...], whitener_ref[:, mine])


def whiten_kernel(core_ref, first_ref, theirs_ref, whitener_ref, out_ref, *, places):
    rows, half = theirs_ref.shape
    theirs = pl.ds(pl.multiple_of((1 - core_ref[0]) * half, half), half)
    white = (first_ref[...] + whiten_half(theirs_ref[...], whitener_ref[:, theirs])).astype(BF16)
    size = out_ref.shape[1] // 2
    n = rows // size
    for q in range(n):
        for e in range(n):
            out_ref[places[q][e], :size, :] = white[e * size : (e + 1) * size]
            out_ref[places[q][e], size:, :] = white[q * size : (q + 1) * size]


def give_kernel(core_ref, pieces_ref, give_ref, rows_ref, cols_ref, *, places):
    count, size, _ = pieces_ref.shape
    size //= 2
    order = [place for line in places for place in line]
    for i, place in enumerate(order):
        rows_ref[i * size : (i + 1) * size, :] = pieces_ref[place, :size, :]
        cols_ref[i * size : (i + 1) * size, :] = pieces_ref[place, size:, :]
    half = give_ref.shape[1]
    theirs = pl.ds(pl.multiple_of((1 - core_ref[0]) * half, half), half)
    give_ref[...] = matmul(rows_ref[...], cols_ref[theirs, :], ((1,), (1,))).astype(BF16)


def keep_kernel(core_ref, rows_ref, cols_ref, keep_ref):
    half = keep_ref.shape[1]
    mine = pl.ds(pl.multiple_of(core_ref[0] * half, half), half)
    keep_ref[...] = matmul(rows_ref[...], cols_ref[mine, :], ((1,), (1,)))


def body(grads, projection, whitener):
    n = lax.axis_size(RING)
    chips = RING + COLS
    core = lax.axis_index("core").astype(jnp.int32).reshape(1)
    sketch_rows = projection.shape[1]
    norm_factor = 1.0 / math.sqrt(grads.shape[0] * n * lax.axis_size("core"))
    width = grads.shape[1]
    half = sketch_rows // 2
    size = width // (n * n)

    own = send_all(spread(whitener, n), ("y_hi", "x")).reshape(half, sketch_rows)

    keep, give = project(core, grads, projection)
    got = lax.ppermute(give, "core", SWAP)
    got, own = lax.optimization_barrier((got, own))
    blocks = (keep + got.astype(F32)).astype(BF16)
    pieces = send_all(blocks.reshape(n * n, size, half), chips)
    shape = jax.ShapeDtypeStruct((n * size, half), F32)
    mine = call(
        lambda *refs: reduce_kernel(*refs, groups=n, scale=norm_factor),
        shape, 0, core, pieces, name="reduce",
    )
    theirs = lax.ppermute(mine, "core", SWAP)
    flops = 4 * n * size * half * half
    shape = jax.ShapeDtypeStruct((n * size, half), F32)
    first = call(first_half_kernel, shape, flops, core, mine, own, name="first_half")
    shape = jax.ShapeDtypeStruct((n * n, 2 * size, half), BF16)
    depth = lax.axis_size("z")
    places = [[(e // depth * n + q) * depth + e % depth for e in range(n)] for q in range(n)]
    copies = call(
        lambda *refs: whiten_kernel(*refs, places=places),
        shape, flops, core, first, theirs, own, name="whiten",
    )
    pieces = send_all(copies, ("y_lo", "x", "y_hi", "z"))
    across = width // lax.axis_size("core")
    flops = 2 * width * across * half
    shapes = (
        jax.ShapeDtypeStruct((width, across), BF16),
        jax.ShapeDtypeStruct((width, half), BF16),
        jax.ShapeDtypeStruct((width, half), BF16),
    )
    give, rows, cols = call(
        lambda *refs: give_kernel(*refs, places=places),
        shapes, flops, core, pieces, name="give",
    )
    got = lax.ppermute(give, "core", SWAP)
    shape = jax.ShapeDtypeStruct((width, across), F32)
    keep = call(keep_kernel, shape, flops, core, rows, cols, name="keep")
    return (keep + got.astype(F32)) * (1.0 / sketch_rows)


def solution(mesh):
    fine = Mesh(mesh.devices.reshape(4, 2, 2, 2, 4), ("x", "y_hi", "core", "y_lo", "z"))
    param = ("x", "y_hi", "core")
    return jax.shard_map(
        body,
        mesh=fine,
        in_specs=(P(param, COLS), P(param, None), P(param, None)),
        out_specs=P(COLS, param),
        check_vma=False,
    )
```

```python
import math

import jax
import jax.numpy as jnp
from jax import lax
from jax.experimental import pallas as pl
from jax.experimental.pallas import tpu as pltpu
from jax.sharding import Mesh, PartitionSpec as P

BF16 = jnp.bfloat16
F32 = jnp.float32
RING = ("x", "y_hi")
COLS = ("y_lo", "z")
SWAP = [(0, 1), (1, 0)]
TILE = 512
STEPS = (1, 2, 3, 3, 2, 1)
TAIL = 3


def matmul(a, b, dims):
    return lax.dot_general(a, b, (dims, ((), ())), preferred_element_type=F32)


def send_all(copies, axes):
    return lax.all_to_all(copies, axes, 0, 0, tiled=True)


def project_kernel(
    core_ref, grads_hbm, projection_hbm, keep_ref, give_ref, grads_tail, projection_tail,
    grads_ref, projection_ref, total, sems,
):
    rows = grads_ref.shape[0]
    half = keep_ref.shape[1]
    head = rows - grads_tail.shape[0]
    mine = pl.ds(pl.multiple_of(core_ref[0] * half, half), half)
    theirs = pl.ds(pl.multiple_of((1 - core_ref[0]) * half, half), half)
    copies = []
    for i in range(rows // TILE):
        part = pl.ds(i * TILE, TILE)
        pair = [pltpu.make_async_copy(grads_hbm.at[part], grads_ref.at[part], sems.at[0, i])]
        if i * TILE < head:
            target = projection_ref.at[part]
            pair.append(pltpu.make_async_copy(projection_hbm.at[part], target, sems.at[1, i]))
        else:
            target = projection_ref.at[part, pl.ds(0, half)]
            source = projection_hbm.at[part, theirs]
            pair.append(pltpu.make_async_copy(source, target, sems.at[1, i]))
            target = projection_tail.at[pl.ds(i * TILE - head, TILE)]
            source = projection_hbm.at[part, mine]
            pair.append(pltpu.make_async_copy(source, target, sems.at[2, i]))
        for copy in pair:
            copy.start()
        copies.append(pair)
    first = 0
    for count in STEPS:
        for pair in copies[first : first + count]:
            for copy in pair:
                copy.wait()
        start = first * TILE
        part = pl.ds(start, count * TILE)
        grads = grads_ref[part, :].astype(BF16)
        first += count
        if start < head:
            near = matmul(grads, projection_ref[part, mine], ((0,), (0,)))
            far = matmul(grads, projection_ref[part, theirs], ((0,), (0,)))
            if start == 0:
                keep_ref[...] = near
                total[...] = far
            else:
                keep_ref[...] += near
                total[...] += far
        else:
            grads_tail[pl.ds(start - head, count * TILE), :] = grads
            far = matmul(grads, projection_ref[part, :half], ((0,), (0,)))
            if first < rows // TILE:
                total[...] += far
            else:
                give_ref[...] = (total[...] + far).astype(BF16)


def project(core, grads, projection):
    rows, width = grads.shape
    cols = projection.shape[1]
    half = cols // 2
    hbm = pl.BlockSpec(memory_space=pl.ANY)
    vmem = pl.BlockSpec(memory_space=pltpu.VMEM)
    return pl.pallas_call(
        project_kernel,
        out_shape=(
            jax.ShapeDtypeStruct((width, half), F32),
            jax.ShapeDtypeStruct((width, half), BF16),
            jax.ShapeDtypeStruct((TAIL * TILE, width), BF16),
            jax.ShapeDtypeStruct((TAIL * TILE, half), projection.dtype),
        ),
        in_specs=[pl.BlockSpec(memory_space=pltpu.SMEM), hbm, hbm],
        out_specs=[vmem] * 4,
        scratch_shapes=[
            pltpu.VMEM((rows, width), grads.dtype),
            pltpu.VMEM((rows, cols), projection.dtype),
            pltpu.VMEM((width, half), F32),
            pltpu.SemaphoreType.DMA((3, rows // TILE)),
        ],
        compiler_params=pltpu.CompilerParams(vmem_limit_bytes=48 << 20),
        cost_estimate=pl.CostEstimate(
            flops=2 * rows * width * cols,
            bytes_accessed=rows * (4 * width + 2 * cols),
            transcendentals=0,
        ),
        name="project",
    )(core, grads, projection)


def tail_kernel(core_ref, keep_ref, grads_ref, projection_ref, out_ref):
    out_ref[...] = keep_ref[...] + matmul(grads_ref[...], projection_ref[...], ((0,), (0,)))


def spread_kernel(part_ref, out_ref):
    part = part_ref[...].astype(BF16)
    for i in range(out_ref.shape[0]):
        out_ref[i] = part


def spread(part, count):
    return pl.pallas_call(
        spread_kernel,
        out_shape=jax.ShapeDtypeStruct((count,) + part.shape, BF16),
        in_specs=[pl.BlockSpec(memory_space=pltpu.VMEM)],
        out_specs=pl.BlockSpec(memory_space=pltpu.VMEM),
        name="spread",
    )(part)


def call(kernel, out_shape, flops, *args, scratch=(), name):
    vmem = pl.BlockSpec(memory_space=pltpu.VMEM)
    moved = sum(a.size * a.dtype.itemsize for a in args[1:])
    return pl.pallas_call(
        kernel,
        out_shape=out_shape,
        in_specs=[pl.BlockSpec(memory_space=pltpu.SMEM)] + [vmem] * (len(args) - 1),
        out_specs=jax.tree.map(lambda _: vmem, out_shape),
        scratch_shapes=scratch,
        compiler_params=pltpu.CompilerParams(vmem_limit_bytes=24 << 20),
        cost_estimate=pl.CostEstimate(flops=flops, bytes_accessed=moved, transcendentals=0),
        name=name,
    )(*args)


def reduce_kernel(core_ref, pieces_ref, out_ref, *, groups, scale):
    count, rows, _ = pieces_ref.shape
    for e in range(groups):
        total = pieces_ref[e].astype(F32)
        for q in range(1, count // groups):
            total += pieces_ref[q * groups + e].astype(F32)
        out_ref[e * rows : (e + 1) * rows, :] = total * scale


def whiten_half(part, block):
    rows = part.shape[0]
    high = part.astype(BF16)
    low = (part - high.astype(F32)).astype(BF16)
    term = matmul(jnp.concatenate([high, low], axis=0), block, ((1,), (1,)))
    return term[:rows] + term[rows:]


def first_half_kernel(core_ref, mine_ref, whitener_ref, out_ref):
    half = mine_ref.shape[1]
    mine = pl.ds(pl.multiple_of(core_ref[0] * half, half), half)
    out_ref[...] = whiten_half(mine_ref[...], whitener_ref[:, mine])


def whiten_kernel(core_ref, first_ref, theirs_ref, whitener_ref, out_ref, *, places):
    rows, half = theirs_ref.shape
    theirs = pl.ds(pl.multiple_of((1 - core_ref[0]) * half, half), half)
    white = (first_ref[...] + whiten_half(theirs_ref[...], whitener_ref[:, theirs])).astype(BF16)
    size = out_ref.shape[1] // 2
    n = rows // size
    for q in range(n):
        for e in range(n):
            out_ref[places[q][e], :size, :] = white[e * size : (e + 1) * size]
            out_ref[places[q][e], size:, :] = white[q * size : (q + 1) * size]


def give_kernel(core_ref, pieces_ref, give_ref, rows_ref, cols_ref, *, places):
    count, size, _ = pieces_ref.shape
    size //= 2
    order = [place for line in places for place in line]
    for i, place in enumerate(order):
        rows_ref[i * size : (i + 1) * size, :] = pieces_ref[place, :size, :]
        cols_ref[i * size : (i + 1) * size, :] = pieces_ref[place, size:, :]
    half = give_ref.shape[1]
    theirs = pl.ds(pl.multiple_of((1 - core_ref[0]) * half, half), half)
    give_ref[...] = matmul(rows_ref[...], cols_ref[theirs, :], ((1,), (1,))).astype(BF16)


def keep_kernel(core_ref, rows_ref, cols_ref, keep_ref):
    half = keep_ref.shape[1]
    mine = pl.ds(pl.multiple_of(core_ref[0] * half, half), half)
    keep_ref[...] = matmul(rows_ref[...], cols_ref[mine, :], ((1,), (1,)))


def body(grads, projection, whitener):
    n = lax.axis_size(RING)
    chips = RING + COLS
    core = lax.axis_index("core").astype(jnp.int32).reshape(1)
    sketch_rows = projection.shape[1]
    norm_factor = 1.0 / math.sqrt(grads.shape[0] * n * lax.axis_size("core"))
    width = grads.shape[1]
    half = sketch_rows // 2
    size = width // (n * n)

    own = send_all(spread(whitener, n), ("y_hi", "x")).reshape(half, sketch_rows)

    keep, give, *tail = project(core, grads, projection)
    got = lax.ppermute(give, "core", SWAP)
    shape = jax.ShapeDtypeStruct(keep.shape, F32)
    flops = 2 * TAIL * TILE * width * half
    keep = call(tail_kernel, shape, flops, core, keep, *tail, name="tail")
    got, own = lax.optimization_barrier((got, own))
    blocks = (keep + got.astype(F32)).astype(BF16)
    pieces = send_all(blocks.reshape(n * n, size, half), chips)
    shape = jax.ShapeDtypeStruct((n * size, half), F32)
    mine = call(
        lambda *refs: reduce_kernel(*refs, groups=n, scale=norm_factor),
        shape, 0, core, pieces, name="reduce",
    )
    theirs = lax.ppermute(mine, "core", SWAP)
    flops = 4 * n * size * half * half
    shape = jax.ShapeDtypeStruct((n * size, half), F32)
    first = call(first_half_kernel, shape, flops, core, mine, own, name="first_half")
    shape = jax.ShapeDtypeStruct((n * n, 2 * size, half), BF16)
    depth = lax.axis_size("z")
    places = [[(e // depth * n + q) * depth + e % depth for e in range(n)] for q in range(n)]
    copies = call(
        lambda *refs: whiten_kernel(*refs, places=places),
        shape, flops, core, first, theirs, own, name="whiten",
    )
    pieces = send_all(copies, ("y_lo", "x", "y_hi", "z"))
    across = width // lax.axis_size("core")
    flops = 2 * width * across * half
    shapes = (
        jax.ShapeDtypeStruct((width, across), BF16),
        jax.ShapeDtypeStruct((width, half), BF16),
        jax.ShapeDtypeStruct((width, half), BF16),
    )
    give, rows, cols = call(
        lambda *refs: give_kernel(*refs, places=places),
        shapes, flops, core, pieces, name="give",
    )
    got = lax.ppermute(give, "core", SWAP)
    shape = jax.ShapeDtypeStruct((width, across), F32)
    keep = call(keep_kernel, shape, flops, core, rows, cols, name="keep")
    return (keep + got.astype(F32)) * (1.0 / sketch_rows)


def solution(mesh):
    fine = Mesh(mesh.devices.reshape(4, 2, 2, 2, 4), ("x", "y_hi", "core", "y_lo", "z"))
    param = ("x", "y_hi", "core")
    return jax.shard_map(
        body,
        mesh=fine,
        in_specs=(P(param, COLS), P(param, None), P(param, None)),
        out_specs=P(COLS, param),
        check_vma=False,
    )
```

```python
import math

import jax
import jax.numpy as jnp
from jax import lax
from jax.experimental import pallas as pl
from jax.experimental.pallas import tpu as pltpu
from jax.sharding import Mesh, PartitionSpec as P

BF16 = jnp.bfloat16
F32 = jnp.float32
RING = ("x", "y_hi")
COLS = ("y_lo", "z")
SWAP = [(0, 1), (1, 0)]
TILE = 512
STEPS = (1, 2, 3, 3, 2, 1)
TAIL = 3


def matmul(a, b, dims):
    return lax.dot_general(a, b, (dims, ((), ())), preferred_element_type=F32)


def send_all(copies, axes):
    return lax.all_to_all(copies, axes, 0, 0, tiled=True)


def project_kernel(
    core_ref, grads_hbm, projection_hbm, keep_ref, give_ref, grads_tail, projection_tail,
    grads_ref, projection_ref, total, sems,
):
    rows = grads_ref.shape[0]
    half = keep_ref.shape[1]
    head = rows - grads_tail.shape[0]
    mine = pl.ds(pl.multiple_of(core_ref[0] * half, half), half)
    theirs = pl.ds(pl.multiple_of((1 - core_ref[0]) * half, half), half)
    copies = []
    for i in range(rows // TILE):
        part = pl.ds(i * TILE, TILE)
        pair = [pltpu.make_async_copy(grads_hbm.at[part], grads_ref.at[part], sems.at[0, i])]
        if i * TILE < head:
            target = projection_ref.at[part]
            pair.append(pltpu.make_async_copy(projection_hbm.at[part], target, sems.at[1, i]))
        else:
            target = projection_ref.at[part, pl.ds(0, half)]
            source = projection_hbm.at[part, theirs]
            pair.append(pltpu.make_async_copy(source, target, sems.at[1, i]))
            target = projection_tail.at[pl.ds(i * TILE - head, TILE)]
            source = projection_hbm.at[part, mine]
            pair.append(pltpu.make_async_copy(source, target, sems.at[2, i]))
        for copy in pair:
            copy.start()
        copies.append(pair)
    first = 0
    for count in STEPS:
        for pair in copies[first : first + count]:
            for copy in pair:
                copy.wait()
        start = first * TILE
        part = pl.ds(start, count * TILE)
        grads = grads_ref[part, :].astype(BF16)
        first += count
        if start < head:
            near = matmul(grads, projection_ref[part, mine], ((0,), (0,)))
            far = matmul(grads, projection_ref[part, theirs], ((0,), (0,)))
            if start == 0:
                keep_ref[...] = near
                total[...] = far
            else:
                keep_ref[...] += near
                total[...] += far
        else:
            grads_tail[pl.ds(start - head, count * TILE), :] = grads
            far = matmul(grads, projection_ref[part, :half], ((0,), (0,)))
            if first < rows // TILE:
                total[...] += far
            else:
                give_ref[...] = (total[...] + far).astype(BF16)


def project(core, grads, projection):
    rows, width = grads.shape
    cols = projection.shape[1]
    half = cols // 2
    hbm = pl.BlockSpec(memory_space=pl.ANY)
    vmem = pl.BlockSpec(memory_space=pltpu.VMEM)
    return pl.pallas_call(
        project_kernel,
        out_shape=(
            jax.ShapeDtypeStruct((width, half), F32),
            jax.ShapeDtypeStruct((width, half), BF16),
            jax.ShapeDtypeStruct((TAIL * TILE, width), BF16),
            jax.ShapeDtypeStruct((TAIL * TILE, half), projection.dtype),
        ),
        in_specs=[pl.BlockSpec(memory_space=pltpu.SMEM), hbm, hbm],
        out_specs=[vmem] * 4,
        scratch_shapes=[
            pltpu.VMEM((rows, width), grads.dtype),
            pltpu.VMEM((rows, cols), projection.dtype),
            pltpu.VMEM((width, half), F32),
            pltpu.SemaphoreType.DMA((3, rows // TILE)),
        ],
        compiler_params=pltpu.CompilerParams(vmem_limit_bytes=48 << 20),
        cost_estimate=pl.CostEstimate(
            flops=2 * rows * width * cols,
            bytes_accessed=rows * (4 * width + 2 * cols),
            transcendentals=0,
        ),
        name="project",
    )(core, grads, projection)


def tail_kernel(core_ref, keep_ref, grads_ref, projection_ref, out_ref):
    out_ref[...] = keep_ref[...] + matmul(grads_ref[...], projection_ref[...], ((0,), (0,)))


def spread_kernel(part_ref, out_ref):
    part = part_ref[...].astype(BF16)
    for i in range(out_ref.shape[0]):
        out_ref[i] = part


def spread(part, count):
    return pl.pallas_call(
        spread_kernel,
        out_shape=jax.ShapeDtypeStruct((count,) + part.shape, BF16),
        in_specs=[pl.BlockSpec(memory_space=pltpu.VMEM)],
        out_specs=pl.BlockSpec(memory_space=pltpu.VMEM),
        name="spread",
    )(part)


def call(kernel, out_shape, flops, *args, scratch=(), name):
    vmem = pl.BlockSpec(memory_space=pltpu.VMEM)
    moved = sum(a.size * a.dtype.itemsize for a in args[1:])
    return pl.pallas_call(
        kernel,
        out_shape=out_shape,
        in_specs=[pl.BlockSpec(memory_space=pltpu.SMEM)] + [vmem] * (len(args) - 1),
        out_specs=jax.tree.map(lambda _: vmem, out_shape),
        scratch_shapes=scratch,
        compiler_params=pltpu.CompilerParams(vmem_limit_bytes=24 << 20),
        cost_estimate=pl.CostEstimate(flops=flops, bytes_accessed=moved, transcendentals=0),
        name=name,
    )(*args)


def reduce_kernel(core_ref, pieces_ref, out_ref, *, groups, scale):
    count, rows, _ = pieces_ref.shape
    for e in range(groups):
        total = pieces_ref[e].astype(F32)
        for q in range(1, count // groups):
            total += pieces_ref[q * groups + e].astype(F32)
        out_ref[e * rows : (e + 1) * rows, :] = total * scale


def whiten_half(part, block):
    rows = part.shape[0]
    high = part.astype(BF16)
    low = (part - high.astype(F32)).astype(BF16)
    term = matmul(jnp.concatenate([high, low], axis=0), block, ((1,), (1,)))
    return term[:rows] + term[rows:]


def first_half_kernel(core_ref, mine_ref, whitener_ref, out_ref):
    half = mine_ref.shape[1]
    mine = pl.ds(pl.multiple_of(core_ref[0] * half, half), half)
    out_ref[...] = whiten_half(mine_ref[...], whitener_ref[:, mine])


def whiten_kernel(core_ref, first_ref, theirs_ref, whitener_ref, out_ref, *, places):
    rows, half = theirs_ref.shape
    theirs = pl.ds(pl.multiple_of((1 - core_ref[0]) * half, half), half)
    white = (first_ref[...] + whiten_half(theirs_ref[...], whitener_ref[:, theirs])).astype(BF16)
    size = out_ref.shape[1] // 2
    n = rows // size
    for q in range(n):
        for e in range(n):
            out_ref[places[q][e], :size, :] = white[e * size : (e + 1) * size]
            out_ref[places[q][e], size:, :] = white[q * size : (q + 1) * size]


def give_kernel(core_ref, pieces_ref, give_ref, rows_ref, cols_ref, *, places):
    count, size, _ = pieces_ref.shape
    size //= 2
    order = [place for line in places for place in line]
    for i, place in enumerate(order):
        rows_ref[i * size : (i + 1) * size, :] = pieces_ref[place, :size, :]
        cols_ref[i * size : (i + 1) * size, :] = pieces_ref[place, size:, :]
    half = give_ref.shape[1]
    theirs = pl.ds(pl.multiple_of((1 - core_ref[0]) * half, half), half)
    give_ref[...] = matmul(rows_ref[...], cols_ref[theirs, :], ((1,), (1,))).astype(BF16)


def keep_kernel(core_ref, rows_ref, cols_ref, keep_ref):
    half = keep_ref.shape[1]
    mine = pl.ds(pl.multiple_of(core_ref[0] * half, half), half)
    keep_ref[...] = matmul(rows_ref[...], cols_ref[mine, :], ((1,), (1,)))


def body(grads, projection, whitener):
    n = lax.axis_size(RING)
    chips = RING + COLS
    core = lax.axis_index("core").astype(jnp.int32).reshape(1)
    sketch_rows = projection.shape[1]
    norm_factor = 1.0 / math.sqrt(grads.shape[0] * n * lax.axis_size("core"))
    width = grads.shape[1]
    half = sketch_rows // 2
    size = width // (n * n)

    own = send_all(spread(whitener, n), RING).reshape(half, sketch_rows)

    keep, give, *tail = project(core, grads, projection)
    got = lax.ppermute(give, "core", SWAP)
    shape = jax.ShapeDtypeStruct(keep.shape, F32)
    flops = 2 * TAIL * TILE * width * half
    keep = call(tail_kernel, shape, flops, core, keep, *tail, name="tail")
    got, own = lax.optimization_barrier((got, own))
    blocks = (keep + got.astype(F32)).astype(BF16)
    pieces = send_all(blocks.reshape(n * n, size, half), chips)
    shape = jax.ShapeDtypeStruct((n * size, half), F32)
    mine = call(
        lambda *refs: reduce_kernel(*refs, groups=n, scale=norm_factor),
        shape, 0, core, pieces, name="reduce",
    )
    theirs = lax.ppermute(mine, "core", SWAP)
    flops = 4 * n * size * half * half
    shape = jax.ShapeDtypeStruct((n * size, half), F32)
    first = call(first_half_kernel, shape, flops, core, mine, own, name="first_half")
    shape = jax.ShapeDtypeStruct((n * n, 2 * size, half), BF16)
    depth = lax.axis_size("z")
    places = [[(e // depth * n + q) * depth + e % depth for e in range(n)] for q in range(n)]
    copies = call(
        lambda *refs: whiten_kernel(*refs, places=places),
        shape, flops, core, first, theirs, own, name="whiten",
    )
    pieces = send_all(copies, ("y_lo", "x", "y_hi", "z"))
    across = width // lax.axis_size("core")
    flops = 2 * width * across * half
    shapes = (
        jax.ShapeDtypeStruct((width, across), BF16),
        jax.ShapeDtypeStruct((width, half), BF16),
        jax.ShapeDtypeStruct((width, half), BF16),
    )
    give, rows, cols = call(
        lambda *refs: give_kernel(*refs, places=places),
        shapes, flops, core, pieces, name="give",
    )
    got = lax.ppermute(give, "core", SWAP)
    shape = jax.ShapeDtypeStruct((width, across), F32)
    keep = call(keep_kernel, shape, flops, core, rows, cols, name="keep")
    return (keep + got.astype(F32)) * (1.0 / sketch_rows)


def solution(mesh):
    fine = Mesh(mesh.devices.reshape(4, 2, 2, 2, 4), ("x", "y_hi", "core", "y_lo", "z"))
    param = ("x", "y_hi", "core")
    return jax.shard_map(
        body,
        mesh=fine,
        in_specs=(P(param, COLS), P(param, None), P(param, None)),
        out_specs=P(COLS, param),
        check_vma=False,
    )
```
